32 devices in a mesh: seq: 8 (over z, y), head: 4 (over x, core).
Axes of the slice: x: 2, y: 2, z: 4, core: 2. Of those that a mesh axis runs over, the one named last changes fastest.
Arguments:
- query: bfloat16 [4096, 8192], P('seq', 'head'), may hold values from -1.5 to 1.5
- key_in: bfloat16 [4096, 8192], P('seq', 'head'), may hold values from -0.5 to 0.5
- value: bfloat16 [4096, 8192], P('seq', 'head'), may hold values from -6 to 6
- gate: bfloat16 [4096, 8192], P(('seq', 'head')), may hold values from -6 to 6
- gain: float32 [8192], replicated, may hold values from 0.5 to 1.5
- grad_out: bfloat16 [4096, 8192], P(('seq', 'head')), may hold values from -6 to 6
Outputs:
- grad_query: bfloat16 [4096, 8192], P('seq', 'head')
- grad_key: bfloat16 [4096, 8192], P('seq', 'head')
- grad_value: bfloat16 [4096, 8192], P('seq', 'head')
- grad_gate: bfloat16 [4096, 8192], P(('seq', 'head'))
The draws below stay inside these ranges and needn't reach their ends.
All inputs are finite; a program needn't handle non-finite values.
Results may differ from the reference program's by a relative error of at most 0.012.
Values may be sent and summed in bfloat16 or wider, within the bound.
A program may use at most 128 MiB of HBM per device.

```python
import jax
import jax.numpy as jnp
from jax import lax

HEADS = 64
HEAD_DIM = 128
TOK_DEV = 512
TOKENS = 4096
WIDTH = 8192
N_SEQ = 8


def block_scale(key, dims, shards, least, high):
    level = 1.0
    for dim, shards_of in shards:
        heights = jax.random.uniform(jax.random.fold_in(jax.random.fold_in(key, 6), dim), (shards_of,), jnp.float32, least / len(shards), high / len(shards))
        level = level * jnp.repeat(jnp.exp(heights), dims[dim] // shards_of).reshape((-1,) + (1,) * (len(dims) - 1 - dim))
    return level


def centred(own_key, shape, deviation, most, split=(), kind=jnp.bfloat16):
    level = block_scale(own_key, shape, split, -0.22, 0.18) if split else 1.0
    entries = jax.random.normal(own_key, shape, jnp.float32) * deviation * level
    return jnp.minimum(jnp.maximum(entries, -most), most).astype(kind)


def setup_inputs(seed: int = 0) -> dict:
    seeds = jax.random.split(jax.random.key(seed), 7)
    return {
        "query": centred(seeds[0], (TOKENS, WIDTH), 0.25, 1.5, ((0, 8), (1, 4))),
        "key_in": centred(seeds[1], (TOKENS, WIDTH), HEAD_DIM ** -0.5, 0.5, ((0, 8), (1, 4))),
        "value": centred(seeds[2], (TOKENS, WIDTH), 1.0, 6.0, ((0, 8), (1, 4))),
        "gate": centred(seeds[3], (TOKENS, WIDTH), 1.0, 6.0, ((0, 32),)),
        "gain": jnp.clip(1.0 + 0.1 * jax.random.normal(seeds[4], (WIDTH,), jnp.float32), 0.5, 1.5),
        "grad_out": centred(seeds[5], (TOKENS, WIDTH), 1.0, 6.0, ((0, 32),)),
    }


def reference(query, key_in, value, gate, gain, grad_out):
    blocks = N_SEQ
    tok_block = TOK_DEV
    width_all = HEADS * HEAD_DIM
    queries = query.reshape(blocks, tok_block, HEADS, HEAD_DIM)
    keys_all = key_in.reshape(blocks, tok_block, HEADS, HEAD_DIM)
    values_all = value.reshape(blocks, tok_block, HEADS, HEAD_DIM)
    block_state = jnp.einsum('bthd,bthe->bhde', keys_all.astype(jnp.float32), values_all.astype(jnp.float32))
    zero_state = jnp.zeros((1, HEADS, HEAD_DIM, HEAD_DIM), jnp.float32)
    prefix = jnp.concatenate([zero_state, jnp.cumsum(block_state[:-1], axis=0)], axis=0)
    causal = jnp.tril(jnp.ones((tok_block, tok_block), dtype=bool))

    def forward_block(operands):
        q_block, k_block, v_block, p_block = operands
        scores = jnp.einsum('thd,shd->hts', q_block.astype(jnp.float32), k_block.astype(jnp.float32))
        masked_scores = jnp.where(causal[None], scores, 0.0).astype(jnp.bfloat16)
        prefix_low = p_block.astype(jnp.bfloat16)
        result = jnp.einsum('hts,she->the', masked_scores.astype(jnp.float32), v_block.astype(jnp.float32))
        result = result + jnp.einsum('thd,hde->the', q_block.astype(jnp.float32), prefix_low.astype(jnp.float32))
        return result.astype(jnp.bfloat16)
    attn_out = lax.map(forward_block, (queries, keys_all, values_all, prefix))
    attn_out = attn_out.reshape(blocks, tok_block, width_all)
    gate_blocks = gate.reshape(blocks, tok_block, width_all)
    grad_blocks = grad_out.reshape(blocks, tok_block, width_all)

    def norm_block(operands):
        out_block, gate_block, grad_block = operands
        rows_wide = out_block.astype(jnp.float32)
        inv_rms = lax.rsqrt(lax.optimization_barrier(jnp.mean(rows_wide * rows_wide, axis=1, keepdims=True)) + 1e-06)
        normed = rows_wide * inv_rms
        gate_wide = gate_block.astype(jnp.float32)
        sigmoid_gate = jax.nn.sigmoid(gate_wide)
        scaled = grad_block.astype(jnp.float32) * gain[None, :]
        grad_gate = (scaled * normed * sigmoid_gate * (1.0 + gate_wide * (1.0 - sigmoid_gate))).astype(jnp.bfloat16)
        weighted = scaled * gate_wide * sigmoid_gate
        grad_attn = inv_rms * (weighted - normed * lax.optimization_barrier(jnp.mean(weighted * normed, axis=1, keepdims=True)))
        return (grad_attn.astype(jnp.bfloat16), grad_gate)
    grad_attn, grad_gate = lax.map(norm_block, (attn_out, gate_blocks, grad_blocks))
    grad_attn = grad_attn.reshape(blocks, tok_block, HEADS, HEAD_DIM)
    block_grad = jnp.einsum('bthd,bthe->bhde', queries.astype(jnp.float32), grad_attn.astype(jnp.float32))
    flipped = jnp.flip(block_grad, axis=0)
    suffix = jnp.flip(jnp.concatenate([zero_state, jnp.cumsum(flipped[:-1], axis=0)], axis=0), axis=0)

    def backward_block(operands):
        q_block, k_block, v_block, do_block, p_block, s_block = operands
        q_wide = q_block.astype(jnp.float32)
        k_wide = k_block.astype(jnp.float32)
        v_wide = v_block.astype(jnp.float32)
        do_wide = do_block.astype(jnp.float32)
        prefix_low = p_block.astype(jnp.bfloat16).astype(jnp.float32)
        suffix_low = s_block.astype(jnp.bfloat16).astype(jnp.float32)
        scores = jnp.einsum('thd,shd->hts', q_wide, k_wide)
        masked_scores = jnp.where(causal[None], scores, 0.0).astype(jnp.bfloat16).astype(jnp.float32)
        grad_scores = jnp.where(causal[None], jnp.einsum('the,she->hts', do_wide, v_wide), 0.0)
        grad_scores = grad_scores.astype(jnp.bfloat16).astype(jnp.float32)
        grad_query = jnp.einsum('hts,shd->thd', grad_scores, k_wide) + jnp.einsum('the,hde->thd', do_wide, prefix_low)
        grad_key = jnp.einsum('hts,thd->shd', grad_scores, q_wide) + jnp.einsum('she,hde->shd', v_wide, suffix_low)
        grad_value = jnp.einsum('hts,the->she', masked_scores, do_wide) + jnp.einsum('shd,hde->she', k_wide, suffix_low)
        return (grad_query.astype(jnp.bfloat16), grad_key.astype(jnp.bfloat16), grad_value.astype(jnp.bfloat16))
    grad_query, grad_key, grad_value = lax.map(backward_block, (queries, keys_all, values_all, grad_attn, prefix, suffix))
    total_rows = blocks * tok_block
    return (grad_query.reshape(total_rows, width_all), grad_key.reshape(total_rows, width_all), grad_value.reshape(total_rows, width_all), grad_gate.reshape(total_rows, width_all))
```

```python
import functools

import jax
import jax.numpy as jnp
from jax import lax
from jax.experimental import pallas as pl
from jax.experimental.pallas import tpu as pltpu
from jax.sharding import PartitionSpec as P

HEAD_DIM = 128
EPS = 1e-06
MESH = pl.DeviceIdType.MESH
F32 = jnp.float32
BF16 = jnp.bfloat16


def dot_nn(a, b):
    return lax.dot_general(a, b, (((1,), (0,)), ((), ())), preferred_element_type=F32)


def dot_nt(a, b):
    return lax.dot_general(a, b, (((1,), (1,)), ((), ())), preferred_element_type=F32)


def dot_tn(a, b):
    return lax.dot_general(a, b, (((0,), (0,)), ((), ())), preferred_element_type=F32)


def body(
    n_seq, n_head,
    q_h, k_h, v_h, gate_h, gain_h, go_h,
    gq_h, gk_h, gv_h, gg_h,
    q, k, v, gate, gain, go,
    wsend, wbuf, g2, attn, d_o, arows,
    st, st_p, st_c, st_o, pre,
    gst, gst_p, gst_c, gst_o,
    zbuf, stat_s, stat_r, inv_b, c_b,
    gqv, gkv, gvv, ggv,
    in_sem, out_sem, gg_sem,
    w_ss, w_rs, a_ss, a_rs, s_ss, s_rs,
    p_ss, p_rs, c_ss, c_rs, gp_ss, gp_rs, gc_ss, gc_rs,
):
    hd = HEAD_DIM
    tok, cols = q.shape
    rows, width = gate.shape
    heads = cols // hd
    half = tok // 2
    idx = lax.axis_index("seq")
    me = lax.axis_index("head")
    side = lax.rem(idx, 2)
    partner = idx + 1 - 2 * side
    has_below = idx >= 2
    has_above = idx + 2 < n_seq
    order = [n_head // 2] + [d for d in range(1, n_head) if d != n_head // 2]

    def to_peer(d):
        return lax.rem(me + d, n_head)

    def from_peer(d):
        return lax.rem(me + n_head - d, n_head)

    loads = [
        pltpu.make_async_copy(src, dst, in_sem.at[i])
        for i, (src, dst) in enumerate(
            ((gain_h, gain), (gate_h, gate), (go_h, go), (k_h, k), (v_h, v), (q_h, q))
        )
    ]
    for load in loads:
        load.start()

    barrier = pltpu.get_barrier_semaphore()
    for d in range(1, n_head):
        pl.semaphore_signal(barrier, inc=1, device_id={"head": to_peer(d)}, device_id_type=MESH)
    pl.semaphore_signal(barrier, inc=1, device_id={"seq": partner}, device_id_type=MESH)

    @pl.when(has_below)
    def _():
        pl.semaphore_signal(barrier, inc=1, device_id={"seq": idx - 2}, device_id_type=MESH)

    @pl.when(has_above)
    def _():
        pl.semaphore_signal(barrier, inc=1, device_id={"seq": idx + 2}, device_id_type=MESH)

    below, above = has_below.astype(jnp.int32), has_above.astype(jnp.int32)
    pl.semaphore_wait(barrier, n_head + below + above)

    def head_cols(h):
        return pl.ds(pl.multiple_of(h * hd, hd), hd)

    br, bc = 32, 512
    n_bc = cols // bc
    n_blocks = (rows // br) * n_bc

    def block_at(i, start):
        r = pl.multiple_of((i // n_bc) * br, br)
        c = lax.rem(i, n_bc) * bc
        return r, pl.multiple_of(c, bc), pl.multiple_of(start + c, bc)

    def weigh(shard, local):
        start = shard * cols

        def step(i, carry):
            r, c, at = block_at(i, start)
            g = gate[pl.ds(r, br), pl.ds(at, bc)].astype(F32)
            scaled = go[pl.ds(r, br), pl.ds(at, bc)].astype(F32) * gain[:, pl.ds(at, bc)]
            sig = jax.nn.sigmoid(g)
            part = scaled * sig
            g2[pl.ds(r, br), pl.ds(at, bc)] = part * (1.0 + g * (1.0 - sig))
            weighted = (part * g).astype(BF16)
            if local:
                wbuf[pl.ds(pl.multiple_of(me * rows + r, br), br), pl.ds(c, bc)] = weighted
            else:
                wsend[pl.ds(r, br), pl.ds(at, bc)] = weighted
            return carry

        lax.fori_loop(0, n_blocks, step, 0)

    def row_block(shard):
        return pl.ds(pl.multiple_of(shard * rows, rows), rows)

    def col_block(shard):
        return pl.ds(pl.multiple_of(shard * cols, cols), cols)

    def w_copy(d):
        return pltpu.make_async_remote_copy(
            src_ref=wsend.at[:, col_block(to_peer(d))],
            dst_ref=wbuf.at[row_block(me), :],
            send_sem=w_ss.at[d], recv_sem=w_rs.at[d],
            device_id={"head": to_peer(d)}, device_id_type=MESH,
        )

    def w_arrival(d):
        return pltpu.make_async_remote_copy(
            src_ref=wsend.at[:, col_block(to_peer(d))],
            dst_ref=wbuf.at[row_block(from_peer(d)), :],
            send_sem=w_ss.at[d], recv_sem=w_rs.at[d],
            device_id={"head": to_peer(d)}, device_id_type=MESH,
        )

    def a_copy(d):
        return pltpu.make_async_remote_copy(
            src_ref=attn.at[row_block(to_peer(d)), :],
            dst_ref=arows.at[:, col_block(me)],
            send_sem=a_ss.at[d], recv_sem=a_rs.at[d],
            device_id={"head": to_peer(d)}, device_id_type=MESH,
        )

    def a_arrival(d):
        return pltpu.make_async_remote_copy(
            src_ref=attn.at[row_block(to_peer(d)), :],
            dst_ref=arows.at[:, col_block(from_peer(d))],
            send_sem=a_ss.at[d], recv_sem=a_rs.at[d],
            device_id={"head": to_peer(d)}, device_id_type=MESH,
        )

    def s_copy(d):
        return pltpu.make_async_remote_copy(
            src_ref=stat_s, dst_ref=stat_r.at[d],
            send_sem=s_ss.at[d], recv_sem=s_rs.at[d],
            device_id={"head": to_peer(d)}, device_id_type=MESH,
        )

    def state_copy(src, dst, ss, rs, h, target):
        return pltpu.make_async_remote_copy(
            src_ref=src.at[h], dst_ref=dst.at[h],
            send_sem=ss.at[h], recv_sem=rs.at[h],
            device_id={"seq": target}, device_id_type=MESH,
        )

    for load in loads[:3]:
        load.wait()
    for d in order[:1]:
        weigh(to_peer(d), False)
        w_copy(d).start()

    for load in loads[3:5]:
        load.wait()

    def send_state(h, carry):
        sl = head_cols(h)
        st[h] = dot_tn(k[:, sl], v[:, sl]).astype(BF16)
        state_copy(st, st_p, p_ss, p_rs, h, partner).start()
        return carry

    lax.fori_loop(0, heads, send_state, 0)

    for d in order[1:]:
        weigh(to_peer(d), False)
        w_copy(d).start()
    weigh(me, True)
    loads[5].wait()

    def pass_on(h, own, mate, chain, out, sems, source_ok, target_ok, target, wants_mate):
        mate_ss, mate_rs, chain_ss, chain_rs = sems
        state_copy(own, mate, mate_ss, mate_rs, h, partner).wait_recv()
        got = mate[h].astype(F32)

        @pl.when(source_ok)
        def _():
            state_copy(out, chain, chain_ss, chain_rs, h, target).wait_recv()

        @pl.when(jnp.logical_not(source_ok))
        def _():
            chain[h] = jnp.zeros((hd, hd), BF16)

        before = chain[h].astype(F32)

        @pl.when(target_ok)
        def _():
            out[h] = (before + got + own[h].astype(F32)).astype(BF16)
            state_copy(out, chain, chain_ss, chain_rs, h, target).start()

        return (before + wants_mate.astype(F32) * got).astype(BF16)

    at_row = lax.broadcasted_iota(jnp.int32, (half, half), 0)
    at_col = lax.broadcasted_iota(jnp.int32, (half, half), 1)

    def lower(x):
        return jnp.where(at_row >= at_col, x, 0.0).astype(BF16)

    def upper(x):
        return jnp.where(at_row <= at_col, x, 0.0).astype(BF16)

    def forward(h, carry):
        sl = head_cols(h)
        q0, q1 = q[:half, sl], q[half:, sl]
        k0, k1 = k[:half, sl], k[half:, sl]
        v0, v1 = v[:half, sl], v[half:, sl]
        o0 = dot_nn(lower(dot_nt(q0, k0)), v0)
        o1 = dot_nn(dot_nt(q1, k0).astype(BF16), v0) + dot_nn(lower(dot_nt(q1, k1)), v1)
        before = pass_on(
            h, st, st_p, st_c, st_o, (p_ss, p_rs, c_ss, c_rs),
            has_below, has_above, idx + 2, side,
        )
        pre[h] = before
        attn[:half, sl] = (o0 + dot_nn(q0, before)).astype(BF16)
        attn[half:, sl] = (o1 + dot_nn(q1, before)).astype(BF16)
        return carry

    lax.fori_loop(0, heads, forward, 0)

    for d in order:
        w_arrival(d).wait_recv()

    lane = lax.broadcasted_iota(jnp.int32, (64, hd), 1)

    def sums(i, carry):
        rs = pl.ds(pl.multiple_of(i * 64, 64), 64)
        squares = jnp.zeros((64, hd), F32)
        crossed = jnp.zeros((64, hd), F32)
        for h in range(heads):
            a = attn[rs, h * hd:(h + 1) * hd].astype(F32)
            w = wbuf[rs, h * hd:(h + 1) * hd].astype(F32)
            squares = squares + a * a
            crossed = crossed + a * w
        s0 = jnp.sum(squares, axis=1, keepdims=True)
        s1 = jnp.sum(crossed, axis=1, keepdims=True)
        zbuf[rs, :] = jnp.where(lane == 0, s0, jnp.where(lane == 1, s1, 0.0))
        return carry

    lax.fori_loop(0, tok // 64, sums, 0)
    stat_s[...] = jnp.transpose(zbuf[...])[:8]
    for d in order:
        s_copy(d).start()
    for d in order:
        a_copy(d).start()
    total = stat_s[...]
    for d in order:
        s_copy(d).wait_recv()
        total = total + stat_r[d]
    spread = jnp.transpose(jnp.concatenate([total, jnp.zeros((hd - 8, tok), F32)], axis=0))
    inv = lax.rsqrt(spread[:, 0:1] / width + EPS)
    inv_b[...] = jnp.broadcast_to(inv, (tok, hd))
    c_b[...] = jnp.broadcast_to(inv * inv * (spread[:, 1:2] / width), (tok, hd))

    def send_grad(h, carry):
        sl = head_cols(h)
        a = attn[:, sl].astype(F32)
        grad = (inv_b[...] * (wbuf[:, sl].astype(F32) - a * c_b[...])).astype(BF16)
        d_o[:, sl] = grad
        gst[h] = dot_tn(q[:, sl], grad).astype(BF16)
        state_copy(gst, gst_p, gp_ss, gp_rs, h, partner).start()
        return carry

    lax.fori_loop(0, heads, send_grad, 0)

    def out_copies(h):
        sl = head_cols(h)
        return [
            pltpu.make_async_copy(src.at[:, sl], dst.at[:, sl], out_sem.at[i, h])
            for i, (src, dst) in enumerate(((gqv, gq_h), (gkv, gk_h), (gvv, gv_h)))
        ]

    def backward(h, carry):
        sl = head_cols(h)
        q0, q1 = q[:half, sl], q[half:, sl]
        k0, k1 = k[:half, sl], k[half:, sl]
        v0, v1 = v[:half, sl], v[half:, sl]
        d0, d1 = d_o[:half, sl], d_o[half:, sl]
        before = pre[h]
        gqv[:half, sl] = (dot_nn(lower(dot_nt(d0, v0)), k0) + dot_nt(d0, before)).astype(BF16)
        gqv[half:, sl] = (
            dot_nn(dot_nt(d1, v0).astype(BF16), k0)
            + dot_nn(lower(dot_nt(d1, v1)), k1)
            + dot_nt(d1, before)
        ).astype(BF16)
        gk0 = dot_nn(upper(dot_nt(v0, d0)), q0) + dot_nn(dot_nt(v0, d1).astype(BF16), q1)
        gk1 = dot_nn(upper(dot_nt(v1, d1)), q1)
        gv0 = dot_nn(upper(dot_nt(k0, q0)), d0) + dot_nn(dot_nt(k0, q1).astype(BF16), d1)
        gv1 = dot_nn(upper(dot_nt(k1, q1)), d1)
        after = pass_on(
            h, gst, gst_p, gst_c, gst_o, (gp_ss, gp_rs, gc_ss, gc_rs),
            has_above, has_below, idx - 2, 1 - side,
        )
        gkv[:half, sl] = (gk0 + dot_nt(v0, after)).astype(BF16)
        gkv[half:, sl] = (gk1 + dot_nt(v1, after)).astype(BF16)
        gvv[:half, sl] = (gv0 + dot_nn(k0, after)).astype(BF16)
        gvv[half:, sl] = (gv1 + dot_nn(k1, after)).astype(BF16)
        for copy in out_copies(h):
            copy.start()
        return carry

    lax.fori_loop(0, heads, backward, 0)

    def gg_copy(shard, d):
        return pltpu.make_async_copy(
            ggv.at[:, col_block(shard)], gg_h.at[:, col_block(shard)], gg_sem.at[d]
        )

    def finish(shard, local):
        start = shard * cols

        def step(i, carry):
            r, c, at = block_at(i, start)
            mine = pl.multiple_of(me * rows + r, br)
            if local:
                a = attn[pl.ds(mine, br), pl.ds(c, bc)]
            else:
                a = arows[pl.ds(r, br), pl.ds(at, bc)]
            scale = inv_b[pl.ds(mine, br), :][:, 0:1]
            ggv[pl.ds(r, br), pl.ds(at, bc)] = (
                g2[pl.ds(r, br), pl.ds(at, bc)] * (a.astype(F32) * scale)
            ).astype(BF16)
            return carry

        lax.fori_loop(0, n_blocks, step, 0)

    finish(me, True)
    gg_copy(me, 0).start()
    for d in order:
        a_arrival(d).wait_recv()
        finish(from_peer(d), False)
        gg_copy(from_peer(d), d).start()

    gg_copy(me, 0).wait()
    for d in order:
        gg_copy(from_peer(d), d).wait()
        w_copy(d).wait_send()
        s_copy(d).wait_send()
        a_copy(d).wait_send()

    def drain(h, carry):
        for copy in out_copies(h):
            copy.wait()
        state_copy(st, st_p, p_ss, p_rs, h, partner).wait_send()
        state_copy(gst, gst_p, gp_ss, gp_rs, h, partner).wait_send()

        @pl.when(has_above)
        def _():
            state_copy(st_o, st_c, c_ss, c_rs, h, idx + 2).wait_send()

        @pl.when(has_below)
        def _():
            state_copy(gst_o, gst_c, gc_ss, gc_rs, h, idx - 2).wait_send()

        return carry

    lax.fori_loop(0, heads, drain, 0)


def on_device(n_seq, n_head, query, key_in, value, gate, gain, grad_out):
    tok, cols = query.shape
    rows, width = gate.shape
    heads = cols // HEAD_DIM
    wide = pltpu.VMEM((tok, cols), BF16)
    thin = pltpu.VMEM((rows, width), BF16)
    state = pltpu.VMEM((heads, HEAD_DIM, HEAD_DIM), BF16)
    token = pltpu.VMEM((tok, HEAD_DIM), F32)
    by_peer = pltpu.SemaphoreType.DMA((n_head,))
    by_head = pltpu.SemaphoreType.DMA((heads,))
    anywhere = pl.BlockSpec(memory_space=pl.ANY)
    return pl.pallas_call(
        functools.partial(body, n_seq, n_head),
        out_shape=[jax.ShapeDtypeStruct((tok, cols), BF16)] * 3
        + [jax.ShapeDtypeStruct((rows, width), BF16)],
        in_specs=[anywhere] * 6,
        out_specs=[anywhere] * 4,
        scratch_shapes=[
            wide, wide, wide, thin, pltpu.VMEM((1, width), F32), thin,
            thin, wide, pltpu.VMEM((rows, width), F32), wide, wide, thin,
            state, state, state, state, state,
            state, state, state, state,
            token, pltpu.VMEM((8, tok), F32), pltpu.VMEM((n_head, 8, tok), F32), token, token,
            wide, wide, wide, thin,
            pltpu.SemaphoreType.DMA((6,)), pltpu.SemaphoreType.DMA((3, heads)), by_peer,
            by_peer, by_peer, by_peer, by_peer, by_peer, by_peer,
            by_head, by_head, by_head, by_head, by_head, by_head, by_head, by_head,
        ],
        compiler_params=pltpu.CompilerParams(
            collective_id=0, has_side_effects=True, vmem_limit_bytes=60 * 2**20
        ),
        name="linear_attention_backward",
    )(query, key_in, value, gate, gain.reshape(1, width), grad_out)


def solution(mesh):
    in_specs = (
        P("seq", "head"),
        P("seq", "head"),
        P("seq", "head"),
        P(("seq", "head"), None),
        P(),
        P(("seq", "head"), None),
    )
    out_specs = (P("seq", "head"), P("seq", "head"), P("seq", "head"), P(("seq", "head"), None))
    return jax.shard_map(
        functools.partial(on_device, mesh.shape["seq"], mesh.shape["head"]),
        mesh=mesh, in_specs=in_specs, out_specs=out_specs, check_vma=False,
    )
```

```python
import functools

import jax
import jax.numpy as jnp
from jax import lax
from jax.experimental import pallas as pl
from jax.experimental.pallas import tpu as pltpu
from jax.sharding import PartitionSpec as P

HEAD_DIM = 128
EPS = 1e-06
MESH = pl.DeviceIdType.MESH
F32 = jnp.float32
BF16 = jnp.bfloat16
FORWARD_LAG = 4
BACKWARD_LAG = 2


def dot_nn(a, b):
    return lax.dot_general(a, b, (((1,), (0,)), ((), ())), preferred_element_type=F32)


def dot_nt(a, b):
    return lax.dot_general(a, b, (((1,), (1,)), ((), ())), preferred_element_type=F32)


def dot_tn(a, b):
    return lax.dot_general(a, b, (((0,), (0,)), ((), ())), preferred_element_type=F32)


def body(
    n_seq, n_head,
    q_h, k_h, v_h, gate_h, gain_h, go_h,
    gqv, gkv, gvv, ggv,
    q, k, v, gate, gain, go,
    wsend, wbuf, g2, attn, d_o, arows,
    st, st_p, st_c, st_o, pre,
    gst, gst_p, gst_c, gst_o,
    suf, scores, acc_a, acc_b,
    zbuf, stat_s, stat_r, inv_b, c_b,
    in_sem,
    w_ss, w_rs, a_ss, a_rs, s_ss, s_rs,
    p_ss, p_rs, c_ss, c_rs, gp_ss, gp_rs, gc_ss, gc_rs,
):
    hd = HEAD_DIM
    tok, cols = q.shape
    rows, width = gate.shape
    heads = cols // hd
    half = tok // 2
    idx = lax.axis_index("seq")
    me = lax.axis_index("head")
    side = lax.rem(idx, 2)
    partner = idx + 1 - 2 * side
    has_below = idx >= 2
    has_above = idx + 2 < n_seq
    order = [n_head // 2] + [d for d in range(1, n_head) if d != n_head // 2]

    def to_peer(d):
        return lax.rem(me + d, n_head)

    def from_peer(d):
        return lax.rem(me + n_head - d, n_head)

    loads = [
        pltpu.make_async_copy(src, dst, in_sem.at[i])
        for i, (src, dst) in enumerate(
            ((gain_h, gain), (gate_h, gate), (go_h, go), (k_h, k), (v_h, v), (q_h, q))
        )
    ]
    for load in loads:
        load.start()

    barrier = pltpu.get_barrier_semaphore()
    for d in range(1, n_head):
        pl.semaphore_signal(barrier, inc=1, device_id={"head": to_peer(d)}, device_id_type=MESH)
    pl.semaphore_signal(barrier, inc=1, device_id={"seq": partner}, device_id_type=MESH)

    @pl.when(has_below)
    def _():
        pl.semaphore_signal(barrier, inc=1, device_id={"seq": idx - 2}, device_id_type=MESH)

    @pl.when(has_above)
    def _():
        pl.semaphore_signal(barrier, inc=1, device_id={"seq": idx + 2}, device_id_type=MESH)

    below, above = has_below.astype(jnp.int32), has_above.astype(jnp.int32)
    pl.semaphore_wait(barrier, n_head + below + above)

    def head_cols(h):
        return pl.ds(pl.multiple_of(h * hd, hd), hd)

    br, bc = 32, 512
    n_bc = cols // bc
    n_blocks = (rows // br) * n_bc

    def block_at(i, start):
        r = pl.multiple_of((i // n_bc) * br, br)
        c = lax.rem(i, n_bc) * bc
        return r, pl.multiple_of(c, bc), pl.multiple_of(start + c, bc)

    def weigh(shard, local):
        start = shard * cols

        def step(i, carry):
            r, c, at = block_at(i, start)
            g = gate[pl.ds(r, br), pl.ds(at, bc)].astype(F32)
            scaled = go[pl.ds(r, br), pl.ds(at, bc)].astype(F32) * gain[:, pl.ds(at, bc)]
            sig = jax.nn.sigmoid(g)
            part = scaled * sig
            g2[pl.ds(r, br), pl.ds(at, bc)] = part * (1.0 + g * (1.0 - sig))
            weighted = (part * g).astype(BF16)
            if local:
                wbuf[pl.ds(pl.multiple_of(me * rows + r, br), br), pl.ds(c, bc)] = weighted
            else:
                wsend[pl.ds(r, br), pl.ds(at, bc)] = weighted
            return carry

        lax.fori_loop(0, n_blocks, step, 0)

    def row_block(shard):
        return pl.ds(pl.multiple_of(shard * rows, rows), rows)

    def col_block(shard):
        return pl.ds(pl.multiple_of(shard * cols, cols), cols)

    def w_copy(d):
        return pltpu.make_async_remote_copy(
            src_ref=wsend.at[:, col_block(to_peer(d))],
            dst_ref=wbuf.at[row_block(me), :],
            send_sem=w_ss.at[d], recv_sem=w_rs.at[d],
            device_id={"head": to_peer(d)}, device_id_type=MESH,
        )

    def w_arrival(d):
        return pltpu.make_async_remote_copy(
            src_ref=wsend.at[:, col_block(to_peer(d))],
            dst_ref=wbuf.at[row_block(from_peer(d)), :],
            send_sem=w_ss.at[d], recv_sem=w_rs.at[d],
            device_id={"head": to_peer(d)}, device_id_type=MESH,
        )

    def a_copy(d):
        return pltpu.make_async_remote_copy(
            src_ref=attn.at[row_block(to_peer(d)), :],
            dst_ref=arows.at[:, col_block(me)],
            send_sem=a_ss.at[d], recv_sem=a_rs.at[d],
            device_id={"head": to_peer(d)}, device_id_type=MESH,
        )

    def a_arrival(d):
        return pltpu.make_async_remote_copy(
            src_ref=attn.at[row_block(to_peer(d)), :],
            dst_ref=arows.at[:, col_block(from_peer(d))],
            send_sem=a_ss.at[d], recv_sem=a_rs.at[d],
            device_id={"head": to_peer(d)}, device_id_type=MESH,
        )

    def s_copy(d):
        return pltpu.make_async_remote_copy(
            src_ref=stat_s, dst_ref=stat_r.at[d],
            send_sem=s_ss.at[d], recv_sem=s_rs.at[d],
            device_id={"head": to_peer(d)}, device_id_type=MESH,
        )

    def state_copy(src, dst, ss, rs, h, target):
        return pltpu.make_async_remote_copy(
            src_ref=src.at[h], dst_ref=dst.at[h],
            send_sem=ss.at[h], recv_sem=rs.at[h],
            device_id={"seq": target}, device_id_type=MESH,
        )

    for load in loads[:3]:
        load.wait()
    for d in order[:1]:
        weigh(to_peer(d), False)
        w_copy(d).start()

    for load in loads[3:5]:
        load.wait()

    def send_state(h, carry):
        sl = head_cols(h)
        st[h] = dot_tn(k[:, sl], v[:, sl]).astype(BF16)
        state_copy(st, st_p, p_ss, p_rs, h, partner).start()
        return carry

    lax.fori_loop(0, heads, send_state, 0)

    for d in order[1:]:
        weigh(to_peer(d), False)
        w_copy(d).start()
    weigh(me, True)
    loads[5].wait()

    def pass_on(h, own, mate, chain, out, sems, source_ok, target_ok, target, wants_mate):
        mate_ss, mate_rs, chain_ss, chain_rs = sems
        state_copy(own, mate, mate_ss, mate_rs, h, partner).wait_recv()
        got = mate[h].astype(F32)

        @pl.when(source_ok)
        def _():
            state_copy(out, chain, chain_ss, chain_rs, h, target).wait_recv()

        @pl.when(jnp.logical_not(source_ok))
        def _():
            chain[h] = jnp.zeros((hd, hd), BF16)

        before = chain[h].astype(F32)

        @pl.when(target_ok)
        def _():
            out[h] = (before + got + own[h].astype(F32)).astype(BF16)
            state_copy(out, chain, chain_ss, chain_rs, h, target).start()

        return (before + wants_mate.astype(F32) * got).astype(BF16)

    at_row = lax.broadcasted_iota(jnp.int32, (half, half), 0)
    at_col = lax.broadcasted_iota(jnp.int32, (half, half), 1)

    def lower(x):
        return jnp.where(at_row >= at_col, x, 0.0).astype(BF16)

    def upper(x):
        return jnp.where(at_row <= at_col, x, 0.0).astype(BF16)

    depth = idx // 2
    pairs = n_seq // 2

    def forward_local(h):
        sl = head_cols(h)
        q0, q1 = q[:half, sl], q[half:, sl]
        k0, k1 = k[:half, sl], k[half:, sl]
        v0, v1 = v[:half, sl], v[half:, sl]
        acc_a[:half, sl] = dot_nn(lower(dot_nt(q0, k0)), v0)
        acc_a[half:, sl] = dot_nn(dot_nt(q1, k0).astype(BF16), v0) + dot_nn(
            lower(dot_nt(q1, k1)), v1
        )
        scores[h, 0] = upper(dot_nt(k0, q0))
        scores[h, 1] = dot_nt(k0, q1).astype(BF16)
        scores[h, 2] = upper(dot_nt(k1, q1))

    def forward(i, carry):
        @pl.when(i < heads)
        def _():
            forward_local(i)

        h = i - FORWARD_LAG * depth

        @pl.when((h >= 0) & (h < heads))
        def _():
            sl = head_cols(h)
            before = pass_on(
                h, st, st_p, st_c, st_o, (p_ss, p_rs, c_ss, c_rs),
                has_below, has_above, idx + 2, side,
            )
            pre[h] = before
            attn[:, sl] = (acc_a[:, sl] + dot_nn(q[:, sl], before)).astype(BF16)

        return carry

    lax.fori_loop(0, heads + FORWARD_LAG * (pairs - 1), forward, 0)

    for d in order:
        w_arrival(d).wait_recv()

    lane = lax.broadcasted_iota(jnp.int32, (64, hd), 1)

    def sums(i, carry):
        rs = pl.ds(pl.multiple_of(i * 64, 64), 64)
        squares = jnp.zeros((64, hd), F32)
        crossed = jnp.zeros((64, hd), F32)
        for h in range(heads):
            a = attn[rs, h * hd:(h + 1) * hd].astype(F32)
            w = wbuf[rs, h * hd:(h + 1) * hd].astype(F32)
            squares = squares + a * a
            crossed = crossed + a * w
        s0 = jnp.sum(squares, axis=1, keepdims=True)
        s1 = jnp.sum(crossed, axis=1, keepdims=True)
        zbuf[rs, :] = jnp.where(lane == 0, s0, jnp.where(lane == 1, s1, 0.0))
        return carry

    lax.fori_loop(0, tok // 64, sums, 0)
    stat_s[...] = jnp.transpose(zbuf[...])[:8]
    for d in order:
        s_copy(d).start()
    for d in order:
        a_copy(d).start()
    total = stat_s[...]
    for d in order:
        s_copy(d).wait_recv()
        total = total + stat_r[d]
    spread = jnp.transpose(jnp.concatenate([total, jnp.zeros((hd - 8, tok), F32)], axis=0))
    inv = lax.rsqrt(spread[:, 0:1] / width + EPS)
    inv_b[...] = jnp.broadcast_to(inv, (tok, hd))
    c_b[...] = jnp.broadcast_to(inv * inv * (spread[:, 1:2] / width), (tok, hd))

    def send_grad(h, carry):
        sl = head_cols(h)
        a = attn[:, sl].astype(F32)
        grad = (inv_b[...] * (wbuf[:, sl].astype(F32) - a * c_b[...])).astype(BF16)
        d_o[:, sl] = grad
        gst[h] = dot_tn(q[:, sl], grad).astype(BF16)
        state_copy(gst, gst_p, gp_ss, gp_rs, h, partner).start()
        return carry

    lax.fori_loop(0, heads, send_grad, 0)

    def backward_local(h):
        sl = head_cols(h)
        q0, q1 = q[:half, sl], q[half:, sl]
        k0, k1 = k[:half, sl], k[half:, sl]
        v0, v1 = v[:half, sl], v[half:, sl]
        d0, d1 = d_o[:half, sl], d_o[half:, sl]
        before = pre[h]
        gqv[:half, sl] = (dot_nn(lower(dot_nt(d0, v0)), k0) + dot_nt(d0, before)).astype(BF16)
        gqv[half:, sl] = (
            dot_nn(dot_nt(d1, v0).astype(BF16), k0)
            + dot_nn(lower(dot_nt(d1, v1)), k1)
            + dot_nt(d1, before)
        ).astype(BF16)
        acc_a[:half, sl] = dot_nn(upper(dot_nt(v0, d0)), q0) + dot_nn(
            dot_nt(v0, d1).astype(BF16), q1
        )
        acc_a[half:, sl] = dot_nn(upper(dot_nt(v1, d1)), q1)
        acc_b[:half, sl] = dot_nn(scores[h, 0], d0) + dot_nn(scores[h, 1], d1)
        acc_b[half:, sl] = dot_nn(scores[h, 2], d1)

    def backward(i, carry):
        @pl.when(i < heads)
        def _():
            backward_local(i)

        for t in range(2):
            h = 2 * (i - BACKWARD_LAG * (pairs - 1 - depth)) + t

            @pl.when((h >= 0) & (h < heads))
            def _():
                suf[h] = pass_on(
                    h, gst, gst_p, gst_c, gst_o, (gp_ss, gp_rs, gc_ss, gc_rs),
                    has_above, has_below, idx - 2, 1 - side,
                )

        return carry

    steps = max(heads, BACKWARD_LAG * (pairs - 1) + (heads + 1) // 2)
    lax.fori_loop(0, steps, backward, 0)

    def add_later(h, carry):
        sl = head_cols(h)
        after = suf[h]
        gkv[:, sl] = (acc_a[:, sl] + dot_nt(v[:, sl], after)).astype(BF16)
        gvv[:, sl] = (acc_b[:, sl] + dot_nn(k[:, sl], after)).astype(BF16)
        return carry

    lax.fori_loop(0, heads, add_later, 0)

    def finish(shard, local):
        start = shard * cols

        def step(i, carry):
            r, c, at = block_at(i, start)
            mine = pl.multiple_of(me * rows + r, br)
            if local:
                a = attn[pl.ds(mine, br), pl.ds(c, bc)]
            else:
                a = arows[pl.ds(r, br), pl.ds(at, bc)]
            scale = inv_b[pl.ds(mine, br), :][:, 0:1]
            ggv[pl.ds(r, br), pl.ds(at, bc)] = (
                g2[pl.ds(r, br), pl.ds(at, bc)] * (a.astype(F32) * scale)
            ).astype(BF16)
            return carry

        lax.fori_loop(0, n_blocks, step, 0)

    finish(me, True)
    for d in order:
        a_arrival(d).wait_recv()
        finish(from_peer(d), False)

    for d in order:
        w_copy(d).wait_send()
        s_copy(d).wait_send()
        a_copy(d).wait_send()

    def drain(h, carry):
        state_copy(st, st_p, p_ss, p_rs, h, partner).wait_send()
        state_copy(gst, gst_p, gp_ss, gp_rs, h, partner).wait_send()

        @pl.when(has_above)
        def _():
            state_copy(st_o, st_c, c_ss, c_rs, h, idx + 2).wait_send()

        @pl.when(has_below)
        def _():
            state_copy(gst_o, gst_c, gc_ss, gc_rs, h, idx - 2).wait_send()

        return carry

    lax.fori_loop(0, heads, drain, 0)


def store(a, b, c, d, a_h, b_h, c_h, d_h, sem):
    copies = [
        pltpu.make_async_copy(src, dst, sem.at[i])
        for i, (src, dst) in enumerate(((a, a_h), (b, b_h), (c, c_h), (d, d_h)))
    ]
    for copy in copies:
        copy.start()
    for copy in copies:
        copy.wait()


def on_device(n_seq, n_head, query, key_in, value, gate, gain, grad_out):
    tok, cols = query.shape
    rows, width = gate.shape
    heads = cols // HEAD_DIM
    wide = pltpu.VMEM((tok, cols), BF16)
    thin = pltpu.VMEM((rows, width), BF16)
    state = pltpu.VMEM((heads, HEAD_DIM, HEAD_DIM), BF16)
    token = pltpu.VMEM((tok, HEAD_DIM), F32)
    by_peer = pltpu.SemaphoreType.DMA((n_head,))
    by_head = pltpu.SemaphoreType.DMA((heads,))
    anywhere = pl.BlockSpec(memory_space=pl.ANY)
    on_chip = pl.BlockSpec(memory_space=pltpu.VMEM)
    sum_of = pltpu.VMEM((tok, cols), F32)
    results = pl.pallas_call(
        functools.partial(body, n_seq, n_head),
        out_shape=[wide, wide, wide, thin],
        in_specs=[anywhere] * 6,
        out_specs=[on_chip] * 4,
        scratch_shapes=[
            wide, wide, wide, thin, pltpu.VMEM((1, width), F32), thin,
            thin, wide, pltpu.VMEM((rows, width), F32), wide, wide, thin,
            state, state, state, state, state,
            state, state, state, state,
            state, pltpu.VMEM((heads, 3, tok // 2, tok // 2), BF16), sum_of, sum_of,
            token, pltpu.VMEM((8, tok), F32), pltpu.VMEM((n_head, 8, tok), F32), token, token,
            pltpu.SemaphoreType.DMA((6,)),
            by_peer, by_peer, by_peer, by_peer, by_peer, by_peer,
            by_head, by_head, by_head, by_head, by_head, by_head, by_head, by_head,
        ],
        compiler_params=pltpu.CompilerParams(
            collective_id=0, has_side_effects=True, vmem_limit_bytes=52 * 2**20
        ),
        name="linear_attention_backward",
    )(query, key_in, value, gate, gain.reshape(1, width), grad_out)
    return pl.pallas_call(
        store,
        out_shape=[jax.ShapeDtypeStruct(x.shape, BF16) for x in results],
        in_specs=[on_chip] * 4,
        out_specs=[anywhere] * 4,
        scratch_shapes=[pltpu.SemaphoreType.DMA((4,))],
        compiler_params=pltpu.CompilerParams(vmem_limit_bytes=2**20),
        name="store_gradients",
    )(*[pltpu.with_memory_space_constraint(x, pltpu.VMEM) for x in results])


def solution(mesh):
    in_specs = (
        P("seq", "head"),
        P("seq", "head"),
        P("seq", "head"),
        P(("seq", "head"), None),
        P(),
        P(("seq", "head"), None),
    )
    out_specs = (P("seq", "head"), P("seq", "head"), P("seq", "head"), P(("seq", "head"), None))
    return jax.shard_map(
        functools.partial(on_device, mesh.shape["seq"], mesh.shape["head"]),
        mesh=mesh, in_specs=in_specs, out_specs=out_specs, check_vma=False,
    )
```

```python
import functools

import jax
import jax.numpy as jnp
from jax import lax
from jax.experimental import pallas as pl
from jax.experimental.pallas import tpu as pltpu
from jax.sharding import PartitionSpec as P

HEAD_DIM = 128
EPS = 1e-06
MESH = pl.DeviceIdType.MESH
F32 = jnp.float32
BF16 = jnp.bfloat16
FORWARD_LAG = 3
BACKWARD_LAG = 3


def dot_nn(a, b):
    return lax.dot_general(a, b, (((1,), (0,)), ((), ())), preferred_element_type=F32)


def dot_nt(a, b):
    return lax.dot_general(a, b, (((1,), (1,)), ((), ())), preferred_element_type=F32)


def dot_tn(a, b):
    return lax.dot_general(a, b, (((0,), (0,)), ((), ())), preferred_element_type=F32)


def body(
    n_seq, n_head,
    q_h, k_h, v_h, gate_h, gain_h, go_h,
    gqv, gkv, gvv, ggv,
    q, k, v, gate, gain, go,
    wsend, wbuf, g2, attn, d_o, arows,
    st, st_p, st_c, st_o, pre,
    gst, gst_p, gst_c, gst_o,
    suf, scores, acc_a, acc_b,
    zbuf, stat_s, stat_r, inv_b, c_b,
    in_sem,
    w_ss, w_rs, a_ss, a_rs, s_ss, s_rs,
    p_ss, p_rs, c_ss, c_rs, gp_ss, gp_rs, gc_ss, gc_rs,
):
    hd = HEAD_DIM
    tok, cols = q.shape
    rows, width = gate.shape
    heads = cols // hd
    half = tok // 2
    idx = lax.axis_index("seq")
    me = lax.axis_index("head")
    side = lax.rem(idx, 2)
    partner = idx + 1 - 2 * side
    has_below = idx >= 2
    has_above = idx + 2 < n_seq
    order = [n_head // 2] + [d for d in range(1, n_head) if d != n_head // 2]

    def to_peer(d):
        return lax.rem(me + d, n_head)

    def from_peer(d):
        return lax.rem(me + n_head - d, n_head)

    loads = [
        pltpu.make_async_copy(src, dst, in_sem.at[i])
        for i, (src, dst) in enumerate(
            ((k_h, k), (v_h, v), (gain_h, gain), (gate_h, gate), (go_h, go), (q_h, q))
        )
    ]
    for load in loads:
        load.start()

    barrier = pltpu.get_barrier_semaphore()
    for d in range(1, n_head):
        pl.semaphore_signal(barrier, inc=1, device_id={"head": to_peer(d)}, device_id_type=MESH)
    pl.semaphore_signal(barrier, inc=1, device_id={"seq": partner}, device_id_type=MESH)

    @pl.when(has_below)
    def _():
        pl.semaphore_signal(barrier, inc=1, device_id={"seq": idx - 2}, device_id_type=MESH)

    @pl.when(has_above)
    def _():
        pl.semaphore_signal(barrier, inc=1, device_id={"seq": idx + 2}, device_id_type=MESH)

    below, above = has_below.astype(jnp.int32), has_above.astype(jnp.int32)
    pl.semaphore_wait(barrier, n_head + below + above)

    def head_cols(h):
        return pl.ds(pl.multiple_of(h * hd, hd), hd)

    br, bc = 32, 512
    n_bc = cols // bc
    n_blocks = (rows // br) * n_bc

    def block_at(i, start):
        r = pl.multiple_of((i // n_bc) * br, br)
        c = lax.rem(i, n_bc) * bc
        return r, pl.multiple_of(c, bc), pl.multiple_of(start + c, bc)

    def weigh(shard, local):
        start = shard * cols

        def step(i, carry):
            r, c, at = block_at(i, start)
            g = gate[pl.ds(r, br), pl.ds(at, bc)].astype(F32)
            scaled = go[pl.ds(r, br), pl.ds(at, bc)].astype(F32) * gain[:, pl.ds(at, bc)]
            sig = jax.nn.sigmoid(g)
            part = scaled * sig
            g2[pl.ds(r, br), pl.ds(at, bc)] = part * (1.0 + g * (1.0 - sig))
            weighted = (part * g).astype(BF16)
            if local:
                wbuf[pl.ds(pl.multiple_of(me * rows + r, br), br), pl.ds(c, bc)] = weighted
            else:
                wsend[pl.ds(r, br), pl.ds(at, bc)] = weighted
            return carry

        lax.fori_loop(0, n_blocks, step, 0)

    def row_block(shard):
        return pl.ds(pl.multiple_of(shard * rows, rows), rows)

    def col_block(shard):
        return pl.ds(pl.multiple_of(shard * cols, cols), cols)

    def w_copy(d):
        return pltpu.make_async_remote_copy(
            src_ref=wsend.at[:, col_block(to_peer(d))],
            dst_ref=wbuf.at[row_block(me), :],
            send_sem=w_ss.at[d], recv_sem=w_rs.at[d],
            device_id={"head": to_peer(d)}, device_id_type=MESH,
        )

    def w_arrival(d):
        return pltpu.make_async_remote_copy(
            src_ref=wsend.at[:, col_block(to_peer(d))],
            dst_ref=wbuf.at[row_block(from_peer(d)), :],
            send_sem=w_ss.at[d], recv_sem=w_rs.at[d],
            device_id={"head": to_peer(d)}, device_id_type=MESH,
        )

    def a_copy(d):
        return pltpu.make_async_remote_copy(
            src_ref=attn.at[row_block(to_peer(d)), :],
            dst_ref=arows.at[:, col_block(me)],
            send_sem=a_ss.at[d], recv_sem=a_rs.at[d],
            device_id={"head": to_peer(d)}, device_id_type=MESH,
        )

    def a_arrival(d):
        return pltpu.make_async_remote_copy(
            src_ref=attn.at[row_block(to_peer(d)), :],
            dst_ref=arows.at[:, col_block(from_peer(d))],
            send_sem=a_ss.at[d], recv_sem=a_rs.at[d],
            device_id={"head": to_peer(d)}, device_id_type=MESH,
        )

    def s_copy(d):
        return pltpu.make_async_remote_copy(
            src_ref=stat_s, dst_ref=stat_r.at[d],
            send_sem=s_ss.at[d], recv_sem=s_rs.at[d],
            device_id={"head": to_peer(d)}, device_id_type=MESH,
        )

    def state_copy(src, dst, ss, rs, h, target):
        return pltpu.make_async_remote_copy(
            src_ref=src.at[h], dst_ref=dst.at[h],
            send_sem=ss.at[h], recv_sem=rs.at[h],
            device_id={"seq": target}, device_id_type=MESH,
        )

    for load in loads[:2]:
        load.wait()

    def send_state(h, carry):
        sl = head_cols(h)
        st[h] = dot_tn(k[:, sl], v[:, sl]).astype(BF16)
        state_copy(st, st_p, p_ss, p_rs, h, partner).start()
        return carry

    lax.fori_loop(0, heads, send_state, 0)

    for load in loads[2:5]:
        load.wait()
    for d in order:
        weigh(to_peer(d), False)
        w_copy(d).start()
    weigh(me, True)
    loads[5].wait()

    def pass_on(h, own, mate, chain, out, sems, source_ok, target_ok, target, wants_mate):
        mate_ss, mate_rs, chain_ss, chain_rs = sems
        state_copy(own, mate, mate_ss, mate_rs, h, partner).wait_recv()
        got = mate[h].astype(F32)

        @pl.when(source_ok)
        def _():
            state_copy(out, chain, chain_ss, chain_rs, h, target).wait_recv()

        @pl.when(jnp.logical_not(source_ok))
        def _():
            chain[h] = jnp.zeros((hd, hd), BF16)

        before = chain[h].astype(F32)

        @pl.when(target_ok)
        def _():
            out[h] = (before + got + own[h].astype(F32)).astype(BF16)
            state_copy(out, chain, chain_ss, chain_rs, h, target).start()

        return (before + wants_mate.astype(F32) * got).astype(BF16)

    at_row = lax.broadcasted_iota(jnp.int32, (half, half), 0)
    at_col = lax.broadcasted_iota(jnp.int32, (half, half), 1)

    def lower(x):
        return jnp.where(at_row >= at_col, x, 0.0).astype(BF16)

    def upper(x):
        return jnp.where(at_row <= at_col, x, 0.0).astype(BF16)

    depth = idx // 2
    pairs = n_seq // 2

    def forward_local(h):
        sl = head_cols(h)
        q0, q1 = q[:half, sl], q[half:, sl]
        k0, k1 = k[:half, sl], k[half:, sl]
        v0, v1 = v[:half, sl], v[half:, sl]
        acc_a[:half, sl] = dot_nn(lower(dot_nt(q0, k0)), v0)
        acc_a[half:, sl] = dot_nn(dot_nt(q1, k0).astype(BF16), v0) + dot_nn(
            lower(dot_nt(q1, k1)), v1
        )
        scores[h, 0] = upper(dot_nt(k0, q0))
        scores[h, 1] = dot_nt(k0, q1).astype(BF16)
        scores[h, 2] = upper(dot_nt(k1, q1))

    def forward(i, carry):
        @pl.when(i < heads)
        def _():
            forward_local(i)

        h = i - FORWARD_LAG * depth

        @pl.when((h >= 0) & (h < heads))
        def _():
            sl = head_cols(h)
            before = pass_on(
                h, st, st_p, st_c, st_o, (p_ss, p_rs, c_ss, c_rs),
                has_below, has_above, idx + 2, side,
            )
            pre[h] = before
            attn[:, sl] = (acc_a[:, sl] + dot_nn(q[:, sl], before)).astype(BF16)

        return carry

    lax.fori_loop(0, heads + FORWARD_LAG * (pairs - 1), forward, 0)

    for d in order:
        w_arrival(d).wait_recv()

    lane = lax.broadcasted_iota(jnp.int32, (64, hd), 1)

    def sums(i, carry):
        rs = pl.ds(pl.multiple_of(i * 64, 64), 64)
        squares = jnp.zeros((64, hd), F32)
        crossed = jnp.zeros((64, hd), F32)
        for h in range(heads):
            a = attn[rs, h * hd:(h + 1) * hd].astype(F32)
            w = wbuf[rs, h * hd:(h + 1) * hd].astype(F32)
            squares = squares + a * a
            crossed = crossed + a * w
        s0 = jnp.sum(squares, axis=1, keepdims=True)
        s1 = jnp.sum(crossed, axis=1, keepdims=True)
        zbuf[rs, :] = jnp.where(lane == 0, s0, jnp.where(lane == 1, s1, 0.0))
        return carry

    lax.fori_loop(0, tok // 64, sums, 0)
    stat_s[...] = jnp.transpose(zbuf[...])[:8]
    for d in order:
        s_copy(d).start()
    for d in order:
        a_copy(d).start()
    total = stat_s[...]
    for d in order:
        s_copy(d).wait_recv()
        total = total + stat_r[d]
    spread = jnp.transpose(jnp.concatenate([total, jnp.zeros((hd - 8, tok), F32)], axis=0))
    inv = lax.rsqrt(spread[:, 0:1] / width + EPS)
    inv_b[...] = jnp.broadcast_to(inv, (tok, hd))
    c_b[...] = jnp.broadcast_to(inv * inv * (spread[:, 1:2] / width), (tok, hd))

    def send_grad(h, carry):
        sl = head_cols(h)
        a = attn[:, sl].astype(F32)
        grad = (inv_b[...] * (wbuf[:, sl].astype(F32) - a * c_b[...])).astype(BF16)
        d_o[:, sl] = grad
        gst[h] = dot_tn(q[:, sl], grad).astype(BF16)
        state_copy(gst, gst_p, gp_ss, gp_rs, h, partner).start()
        return carry

    lax.fori_loop(0, heads, send_grad, 0)

    def backward_local(h):
        sl = head_cols(h)
        q0, q1 = q[:half, sl], q[half:, sl]
        k0, k1 = k[:half, sl], k[half:, sl]
        v0, v1 = v[:half, sl], v[half:, sl]
        d0, d1 = d_o[:half, sl], d_o[half:, sl]
        before = pre[h]
        gqv[:half, sl] = (dot_nn(lower(dot_nt(d0, v0)), k0) + dot_nt(d0, before)).astype(BF16)
        gqv[half:, sl] = (
            dot_nn(dot_nt(d1, v0).astype(BF16), k0)
            + dot_nn(lower(dot_nt(d1, v1)), k1)
            + dot_nt(d1, before)
        ).astype(BF16)
        acc_a[:half, sl] = dot_nn(upper(dot_nt(v0, d0)), q0) + dot_nn(
            dot_nt(v0, d1).astype(BF16), q1
        )
        acc_a[half:, sl] = dot_nn(upper(dot_nt(v1, d1)), q1)
        acc_b[:half, sl] = dot_nn(scores[h, 0], d0) + dot_nn(scores[h, 1], d1)
        acc_b[half:, sl] = dot_nn(scores[h, 2], d1)

    def backward(i, carry):
        @pl.when(i < heads)
        def _():
            backward_local(i)

        for t in range(2):
            h = 2 * (i - BACKWARD_LAG * (pairs - 1 - depth)) + t

            @pl.when((h >= 0) & (h < heads))
            def _():
                suf[h] = pass_on(
                    h, gst, gst_p, gst_c, gst_o, (gp_ss, gp_rs, gc_ss, gc_rs),
                    has_above, has_below, idx - 2, 1 - side,
                )

        return carry

    steps = max(heads, BACKWARD_LAG * (pairs - 1) + (heads + 1) // 2)
    lax.fori_loop(0, steps, backward, 0)

    def add_later(h, carry):
        sl = head_cols(h)
        after = suf[h]
        gkv[:, sl] = (acc_a[:, sl] + dot_nt(v[:, sl], after)).astype(BF16)
        gvv[:, sl] = (acc_b[:, sl] + dot_nn(k[:, sl], after)).astype(BF16)
        return carry

    lax.fori_loop(0, heads, add_later, 0)

    def finish(shard, local):
        start = shard * cols

        def step(i, carry):
            r, c, at = block_at(i, start)
            mine = pl.multiple_of(me * rows + r, br)
            if local:
                a = attn[pl.ds(mine, br), pl.ds(c, bc)]
            else:
                a = arows[pl.ds(r, br), pl.ds(at, bc)]
            scale = inv_b[pl.ds(mine, br), :][:, 0:1]
            ggv[pl.ds(r, br), pl.ds(at, bc)] = (
                g2[pl.ds(r, br), pl.ds(at, bc)] * (a.astype(F32) * scale)
            ).astype(BF16)
            return carry

        lax.fori_loop(0, n_blocks, step, 0)

    finish(me, True)
    for d in order:
        a_arrival(d).wait_recv()
        finish(from_peer(d), False)

    for d in order:
        w_copy(d).wait_send()
        s_copy(d).wait_send()
        a_copy(d).wait_send()

    def drain(h, carry):
        state_copy(st, st_p, p_ss, p_rs, h, partner).wait_send()
        state_copy(gst, gst_p, gp_ss, gp_rs, h, partner).wait_send()

        @pl.when(has_above)
        def _():
            state_copy(st_o, st_c, c_ss, c_rs, h, idx + 2).wait_send()

        @pl.when(has_below)
        def _():
            state_copy(gst_o, gst_c, gc_ss, gc_rs, h, idx - 2).wait_send()

        return carry

    lax.fori_loop(0, heads, drain, 0)


def store(a, b, c, d, a_h, b_h, c_h, d_h, sem):
    copies = [
        pltpu.make_async_copy(src, dst, sem.at[i])
        for i, (src, dst) in enumerate(((a, a_h), (b, b_h), (c, c_h), (d, d_h)))
    ]
    for copy in copies:
        copy.start()
    for copy in copies:
        copy.wait()


def on_device(n_seq, n_head, query, key_in, value, gate, gain, grad_out):
    tok, cols = query.shape
    rows, width = gate.shape
    heads = cols // HEAD_DIM
    wide = pltpu.VMEM((tok, cols), BF16)
    thin = pltpu.VMEM((rows, width), BF16)
    state = pltpu.VMEM((heads, HEAD_DIM, HEAD_DIM), BF16)
    token = pltpu.VMEM((tok, HEAD_DIM), F32)
    by_peer = pltpu.SemaphoreType.DMA((n_head,))
    by_head = pltpu.SemaphoreType.DMA((heads,))
    anywhere = pl.BlockSpec(memory_space=pl.ANY)
    on_chip = pl.BlockSpec(memory_space=pltpu.VMEM)
    sum_of = pltpu.VMEM((tok, cols), F32)
    results = pl.pallas_call(
        functools.partial(body, n_seq, n_head),
        out_shape=[wide, wide, wide, thin],
        in_specs=[anywhere] * 6,
        out_specs=[on_chip] * 4,
        scratch_shapes=[
            wide, wide, wide, thin, pltpu.VMEM((1, width), F32), thin,
            thin, wide, pltpu.VMEM((rows, width), F32), wide, wide, thin,
            state, state, state, state, state,
            state, state, state, state,
            state, pltpu.VMEM((heads, 3, tok // 2, tok // 2), BF16), sum_of, sum_of,
            token, pltpu.VMEM((8, tok), F32), pltpu.VMEM((n_head, 8, tok), F32), token, token,
            pltpu.SemaphoreType.DMA((6,)),
            by_peer, by_peer, by_peer, by_peer, by_peer, by_peer,
            by_head, by_head, by_head, by_head, by_head, by_head, by_head, by_head,
        ],
        compiler_params=pltpu.CompilerParams(
            collective_id=0, has_side_effects=True, vmem_limit_bytes=52 * 2**20
        ),
        name="linear_attention_backward",
    )(query, key_in, value, gate, gain.reshape(1, width), grad_out)
    return pl.pallas_call(
        store,
        out_shape=[jax.ShapeDtypeStruct(x.shape, BF16) for x in results],
        in_specs=[on_chip] * 4,
        out_specs=[anywhere] * 4,
        scratch_shapes=[pltpu.SemaphoreType.DMA((4,))],
        compiler_params=pltpu.CompilerParams(vmem_limit_bytes=2**20),
        name="store_gradients",
    )(*[pltpu.with_memory_space_constraint(x, pltpu.VMEM) for x in results])


def solution(mesh):
    in_specs = (
        P("seq", "head"),
        P("seq", "head"),
        P("seq", "head"),
        P(("seq", "head"), None),
        P(),
        P(("seq", "head"), None),
    )
    out_specs = (P("seq", "head"), P("seq", "head"), P("seq", "head"), P(("seq", "head"), None))
    return jax.shard_map(
        functools.partial(on_device, mesh.shape["seq"], mesh.shape["head"]),
        mesh=mesh, in_specs=in_specs, out_specs=out_specs, check_vma=False,
    )
```
